512 devices in a mesh: seq: 32 (over y_hi, x, core), head: 16 (over z, y_lo).
Axes of the slice: x: 4, y: 8 (y_hi: 4, y_lo: 2; y = y_hi * 2 + y_lo), z: 8, core: 2. Of those that a mesh axis runs over, the one named last changes fastest.
Arguments:
- queries: bfloat16 [12288, 32, 128], P(('seq', 'head')), may hold values from -8 to 8
- keys: bfloat16 [12288, 16, 128], P(('seq', 'head')), may hold values from -8 to 8
- values: bfloat16 [12288, 16, 128], P(('seq', 'head')), may hold values from -6 to 6
- output_gradient: bfloat16 [12288, 32, 128], P(('seq', 'head')), may hold values from -6 to 6
- doc_lengths: int32 [8], replicated, may hold values from 1 to 9216, 12288 in all
Outputs:
- query_grad: bfloat16 [12288, 32, 128], P(('seq', 'head'))
- key_grad: bfloat16 [12288, 16, 128], P(('seq', 'head'))
- value_grad: bfloat16 [12288, 16, 128], P(('seq', 'head'))
The draws below stay inside these ranges and needn't reach their ends.
Inputs may be any that keep to these rules, and one draw needn't show every extreme that they name: `doc_lengths`: the lengths sum to 12288; the longest has exactly 9216 tokens.
All inputs are finite; a program needn't handle non-finite values.
Results may differ from the reference program's by a relative error of at most 0.02.
Values may be sent and summed in bfloat16 or wider, within the bound.
A program may use at most 64 MiB of HBM per device.

```python
import math
import jax
import jax.numpy as jnp
import numpy as np
from jax import lax

QUERY_HEADS = 32
KEY_VALUE_HEADS = 16
HEAD_SIZE = 128
WINDOW = 4096
ROWS = 384
DOCS = 8
SEQUENCE_TOKENS = 12288


def paired_draw(key):
    new_q = jnp.clip(jax.random.normal(jax.random.fold_in(key, 11), (SEQUENCE_TOKENS, QUERY_HEADS, HEAD_SIZE), jnp.float32), -6.0, 6.0)
    updated_key = jnp.clip(jax.random.normal(jax.random.fold_in(key, 12), (SEQUENCE_TOKENS, KEY_VALUE_HEADS, HEAD_SIZE), jnp.float32), -6.0, 6.0)
    return (new_q, updated_key)


def draw_queries(key, part):
    return paired_draw(key)[0].astype(jnp.bfloat16)


def draw_keys(key, part):
    return paired_draw(key)[1].astype(jnp.bfloat16)


def block_scale(own_key, shape, cuts, low, high):
    loudness, own = 1.0, jax.random.fold_in(own_key, 6)
    for dim, shards_of in cuts:
        steps = jnp.exp(jax.random.uniform(jax.random.fold_in(own, dim), (shards_of,), jnp.float32, low / len(cuts), high / len(cuts)))
        loudness = loudness * jnp.repeat(steps, shape[dim] // shards_of).reshape([-1 if axis == dim else 1 for axis in range(len(shape))])
    return loudness


def length_profile(number_of, total, limit, lean):
    portions = [(1 << 20) // math.isqrt(rank ** lean) + 1 for rank in range(2, number_of + 1)]
    spare, counts = total - limit - (number_of - 1), [1] * (number_of - 1)
    while spare > 0:
        candidates = [i for i in range(number_of - 1) if counts[i] < limit]
        pool, budget = sum([portions[i] for i in candidates]), spare
        for i in candidates:
            more = min(limit - counts[i], max(1, budget * portions[i] // pool), spare)
            counts[i] = counts[i] + more
            spare = spare - more
    return np.array([limit] + counts)


def ragged_sizes(stream_key, count, total, limit, slope):
    if count == 2:
        one = jax.random.randint(stream_key, (), max(1, total - limit), min(limit, total - 1) + 1)
        return jnp.stack([one, total - one])
    tallies = jnp.asarray(length_profile(count, total, limit, slope), jnp.int32)
    twos = (count - 1) // 2
    giver, sink = tallies[1:1 + 2 * twos:2], tallies[2:2 + 2 * twos:2]
    margin = jnp.minimum(giver - 1, limit - sink)
    moved = jax.random.randint(jax.random.fold_in(stream_key, 1), (twos,), 0, 1 << 20) % (margin + 1)
    tallies = tallies.at[1:1 + 2 * twos:2].set(giver - moved).at[2:2 + 2 * twos:2].set(sink + moved)
    return tallies[jax.random.permutation(jax.random.fold_in(stream_key, 2), count)]


def normal_values(key, extent, spread, most, split=(), held_as=jnp.bfloat16):
    factor_of = block_scale(key, extent, split, -0.22, 0.18) if split else 1.0
    values = jax.random.normal(key, extent, jnp.float32) * spread * factor_of
    return jnp.minimum(jnp.maximum(values, -most), most).astype(held_as)


def setup_inputs(seed: int = 0) -> dict:
    key_of = jax.random.split(jax.random.key(seed), 6)
    queries = draw_queries(jax.random.fold_in(key_of[5], 71), 0)
    keys = draw_keys(jax.random.fold_in(key_of[5], 71), 0)
    values = normal_values(key_of[2], (SEQUENCE_TOKENS, KEY_VALUE_HEADS, HEAD_SIZE), 1.0, 6.0, ((0, 512),))
    output_gradient = normal_values(key_of[3], (SEQUENCE_TOKENS, QUERY_HEADS, HEAD_SIZE), 1.0, 6.0, ((0, 512),))
    doc_lengths = ragged_sizes(key_of[4], DOCS, SEQUENCE_TOKENS, SEQUENCE_TOKENS * 3 // 4, 2).astype(jnp.int32)
    return {"queries": queries, "keys": keys, "values": values, "output_gradient": output_gradient, "doc_lengths": doc_lengths}


score_scale = 144.0 ** -0.5
masked_value = -1.0e30


def doc_index(ends, positions):
    return jnp.sum((positions[:, None] >= ends[None, :-1]).astype(jnp.int32), axis=1)


def rounded(value):
    return lax.optimization_barrier(value.astype(jnp.bfloat16)).astype(jnp.float32)


def reference(queries, keys, values, output_gradient, doc_lengths):
    group_width = QUERY_HEADS // KEY_VALUE_HEADS
    reach_blocks = (WINDOW - 1) // ROWS + 1
    span_len = (reach_blocks + 1) * ROWS
    padding_length = reach_blocks * ROWS
    block_count = SEQUENCE_TOKENS // ROWS
    ends = jnp.cumsum(doc_lengths).astype(jnp.int32)
    key_padding = jnp.concatenate([jnp.zeros((padding_length, KEY_VALUE_HEADS, HEAD_SIZE), keys.dtype), keys], axis=0)
    value_padding = jnp.concatenate([jnp.zeros((padding_length, KEY_VALUE_HEADS, HEAD_SIZE), values.dtype), values], axis=0)
    query_head_count = queries.reshape(SEQUENCE_TOKENS, KEY_VALUE_HEADS, group_width, HEAD_SIZE)
    head_gradients = output_gradient.reshape(SEQUENCE_TOKENS, KEY_VALUE_HEADS, group_width, HEAD_SIZE)

    def one_block(carry, block):
        key_sum, value_sum = carry
        start = (block * ROWS).astype(jnp.int32)
        q_blk = jnp.moveaxis(lax.dynamic_slice_in_dim(query_head_count, start, ROWS, 0).astype(jnp.float32), 1, 0)
        g_blk = jnp.moveaxis(lax.dynamic_slice_in_dim(head_gradients, start, ROWS, 0).astype(jnp.float32), 1, 0)
        k_blk = jnp.moveaxis(lax.dynamic_slice_in_dim(key_padding, start, span_len, 0).astype(jnp.float32), 1, 0)
        v_blk = jnp.moveaxis(lax.dynamic_slice_in_dim(value_padding, start, span_len, 0).astype(jnp.float32), 1, 0)
        q_pos = start + jnp.arange(ROWS, dtype=jnp.int32)
        k_pos = start - padding_length + jnp.arange(span_len, dtype=jnp.int32)
        q_doc = doc_index(ends, q_pos)
        k_doc = doc_index(ends, k_pos)
        allowed = (k_pos[None, :] >= 0) & (q_pos[:, None] >= k_pos[None, :])
        allowed = allowed & (q_pos[:, None] - k_pos[None, :] < WINDOW) & (q_doc[:, None] == k_doc[None, :])

        def one_head(items):
            q_head, g_head, k_head, v_head = items
            scores = jnp.einsum('igd,jd->gij', q_head, k_head) * score_scale
            kept = jnp.where(allowed, scores, masked_value)
            top = jnp.max(kept, axis=-1, keepdims=True)
            total = jnp.sum(jnp.where(allowed, jnp.exp(kept - top), 0.0), axis=-1, keepdims=True)
            log_total = top + jnp.log(total)
            probs = jnp.where(allowed, jnp.exp(kept - log_total), 0.0)
            probs_low = rounded(probs)
            output = jnp.einsum('gij,jd->igd', probs_low, v_head)
            delta = jnp.einsum('igd,igd->gi', g_head, output)
            prob_grad = jnp.einsum('igd,jd->gij', g_head, v_head)
            score_grad = rounded(probs * (prob_grad - delta[..., None]))
            q_grad = jnp.einsum('gij,jd->igd', score_grad, k_head) * score_scale
            k_part = jnp.einsum('gij,igd->jd', score_grad, q_head) * score_scale
            v_part = jnp.einsum('gij,igd->jd', probs_low, g_head)
            return q_grad, k_part, v_part

        q_grad, k_part, v_part = lax.map(one_head, (q_blk, g_blk, k_blk, v_blk))
        q_grad = jnp.moveaxis(q_grad, 0, 1)
        k_part = jnp.moveaxis(k_part, 0, 1)
        v_part = jnp.moveaxis(v_part, 0, 1)
        key_sum = lax.dynamic_update_slice_in_dim(key_sum, lax.dynamic_slice_in_dim(key_sum, start, span_len, 0) + k_part, start, 0)
        value_sum = lax.dynamic_update_slice_in_dim(value_sum, lax.dynamic_slice_in_dim(value_sum, start, span_len, 0) + v_part, start, 0)
        return (key_sum, value_sum), q_grad.astype(jnp.bfloat16)

    empty_block = jnp.zeros((padding_length + SEQUENCE_TOKENS, KEY_VALUE_HEADS, HEAD_SIZE), jnp.float32)
    (key_sum, value_sum), q_grads = lax.scan(one_block, (empty_block, empty_block), jnp.arange(block_count, dtype=jnp.int32))
    query_grad = q_grads.reshape(SEQUENCE_TOKENS, QUERY_HEADS, HEAD_SIZE)
    return query_grad, key_sum[padding_length:].astype(jnp.bfloat16), value_sum[padding_length:].astype(jnp.bfloat16)
```

```python
import math

import jax
import jax.numpy as jnp
from jax import lax
from jax.experimental import pallas as pl
from jax.experimental.pallas import tpu as pltpu
from jax.sharding import PartitionSpec as P

WINDOW = 4096

score_scale = 144.0 ** (-0.5)
exp2_scale = score_scale * math.log2(math.e)
masked_value = -1e30


def attention_kernel(
    base_ref, lo_ref, pos_ref, x_ref, kv_hbm, dq_ref, dkv_ref, kv_ref, s_ref, dp_ref, sem
):
    rows = x_ref.shape[0]
    tiles, _, wide = s_ref.shape
    dim = kv_ref.shape[1] // 2
    base = pl.multiple_of(base_ref[0], rows)
    copy = pltpu.make_async_copy(kv_hbm.at[pl.ds(base, tiles * rows), :], kv_ref, sem)
    copy.start()
    q = jnp.concatenate([x_ref[:, :dim], x_ref[:, dim : 2 * dim]], axis=0)
    g = jnp.concatenate([x_ref[:, 2 * dim : 3 * dim], x_ref[:, 3 * dim : 4 * dim]], axis=0)
    lo = lo_ref[...]
    pos = pos_ref[...]
    copy.wait()

    def first(t, top):
        k_tile = kv_ref[pl.ds(pl.multiple_of(t * rows, rows), rows), :dim]
        s = lax.dot_general(k_tile, q, (((1,), (1,)), ((), ())), preferred_element_type=jnp.float32)
        k_pos = base + t * rows + lax.broadcasted_iota(jnp.int32, (rows, wide), 0)
        s = jnp.where((k_pos >= lo) & (k_pos <= pos), s, masked_value)
        s_ref[t] = s
        return jnp.maximum(top, jnp.max(s, axis=0, keepdims=True))

    top = lax.fori_loop(0, tiles, first, jnp.full((1, wide), masked_value, jnp.float32))
    top = top * exp2_scale

    def second(t, state):
        total, delta = state
        v_tile = kv_ref[pl.ds(pl.multiple_of(t * rows, rows), rows), dim:]
        dp = lax.dot_general(
            v_tile, g, (((1,), (1,)), ((), ())), preferred_element_type=jnp.float32
        )
        p = jnp.exp2(s_ref[t] * exp2_scale - top)
        s_ref[t] = p
        dp_ref[t] = dp
        return (
            total + jnp.sum(p, axis=0, keepdims=True),
            delta + jnp.sum(p * dp, axis=0, keepdims=True),
        )

    zero = jnp.zeros((1, wide), jnp.float32)
    total, delta = lax.fori_loop(0, tiles, second, (zero, zero))
    inverse = 1.0 / total
    delta = delta * inverse
    column = jnp.transpose(jnp.broadcast_to(inverse, (dim, wide)))
    g_low = (g.astype(jnp.float32) * column).astype(jnp.bfloat16)
    q_low = (q.astype(jnp.float32) * (column * score_scale)).astype(jnp.bfloat16)

    def third(t, dq):
        at = pl.ds(pl.multiple_of(t * rows, rows), rows)
        p = s_ref[t]
        ds = (p * (dp_ref[t] - delta)).astype(jnp.bfloat16)
        dv = jnp.dot(p.astype(jnp.bfloat16), g_low, preferred_element_type=jnp.float32)
        dk = jnp.dot(ds, q_low, preferred_element_type=jnp.float32)
        dkv_ref[at, :dim] = dk.astype(jnp.bfloat16)
        dkv_ref[at, dim:] = dv.astype(jnp.bfloat16)
        return dq + lax.dot_general(
            kv_ref[at, :dim], ds, (((0,), (0,)), ((), ())), preferred_element_type=jnp.float32
        )

    dq = lax.fori_loop(0, tiles, third, jnp.zeros((dim, wide), jnp.float32))
    dq = jnp.transpose(dq * (inverse * score_scale)).astype(jnp.bfloat16)
    dq_ref[:, :dim] = dq[:rows]
    dq_ref[:, dim:] = dq[rows:]


def body(queries, keys, values, output_gradient, doc_lengths):
    chunk, kv_heads, dim = keys.shape
    group = queries.shape[1] // kv_heads
    seq_count = lax.axis_size("seq")
    my_index = lax.axis_index("seq")
    packed = jnp.concatenate(
        [
            queries.reshape(chunk, kv_heads, group * dim),
            output_gradient.reshape(chunk, kv_heads, group * dim),
            keys,
            values,
        ],
        axis=2,
    )
    local = lax.all_to_all(packed, "head", split_axis=1, concat_axis=0, tiled=True)
    rows = local.shape[0]
    local = local.reshape(rows, local.shape[2])
    kv_all = lax.all_gather(local[:, 2 * group * dim :], "seq", axis=0, tiled=True)
    reach = min((WINDOW - 1) // rows + 1, seq_count - 1)
    tiles = reach + 1
    base = jnp.clip(my_index - reach, 0, seq_count - tiles) * rows
    pos = my_index * rows + jnp.arange(rows, dtype=jnp.int32)
    ends = jnp.cumsum(doc_lengths)
    doc_start = jnp.max(jnp.where(ends[None, :] <= pos[:, None], ends[None, :], 0), axis=1)
    lo = jnp.maximum(doc_start, pos - (WINDOW - 1))
    wide = group * rows
    lo = jnp.tile(lo, group).reshape(1, wide).astype(jnp.int32)
    pos = jnp.tile(pos, group).reshape(1, wide)
    vmem = pl.BlockSpec(memory_space=pltpu.VMEM)
    dq, dkv = pl.pallas_call(
        attention_kernel,
        out_shape=(
            jax.ShapeDtypeStruct((rows, group * dim), jnp.bfloat16),
            jax.ShapeDtypeStruct((tiles * rows, 2 * dim), jnp.bfloat16),
        ),
        in_specs=[
            pl.BlockSpec(memory_space=pltpu.SMEM),
            vmem,
            vmem,
            vmem,
            pl.BlockSpec(memory_space=pl.ANY),
        ],
        out_specs=(vmem, vmem),
        scratch_shapes=[
            pltpu.VMEM((tiles * rows, 2 * dim), jnp.bfloat16),
            pltpu.VMEM((tiles, rows, wide), jnp.float32),
            pltpu.VMEM((tiles, rows, wide), jnp.float32),
            pltpu.SemaphoreType.DMA,
        ],
        compiler_params=pltpu.CompilerParams(vmem_limit_bytes=60 * 2**20),
        name="attention_backward",
    )(base.reshape(1).astype(jnp.int32), lo, pos, local[:, : 2 * group * dim], kv_all)
    spread = jnp.zeros((seq_count * rows, 2 * dim), jnp.bfloat16)
    spread = lax.dynamic_update_slice_in_dim(spread, dkv, base, axis=0)
    own = lax.psum_scatter(spread, "seq", scatter_dimension=0, tiled=True)
    back = jnp.concatenate([dq, own], axis=1).reshape(rows, 1, (group + 2) * dim)
    back = lax.all_to_all(back, "head", split_axis=0, concat_axis=1, tiled=True)
    return (
        back[:, :, : group * dim].reshape(queries.shape),
        back[:, :, group * dim : (group + 1) * dim],
        back[:, :, (group + 1) * dim :],
    )


def solution(mesh):
    spec = P(("seq", "head"), None, None)
    return jax.shard_map(
        body,
        mesh=mesh,
        in_specs=(spec, spec, spec, spec, P()),
        out_specs=(spec, spec, spec),
        check_vma=False,
    )
```

```python
import math

import jax
import jax.numpy as jnp
from jax import lax
from jax.experimental import pallas as pl
from jax.experimental.pallas import tpu as pltpu
from jax.sharding import PartitionSpec as P

WINDOW = 4096

score_scale = 144.0 ** (-0.5)
exp2_scale = score_scale * math.log2(math.e)
masked_value = -1e30


def attention_kernel(
    lo_ref, pos_ref, x_ref, out_ref,
    kv_ref, s_ref, dp_ref, dq_ref, odd_ref, even_ref, pair_ref, got_ref, row_ref,
    partner_send, across_send, chip_send, slot_recv, odd_send, even_send, pair_recv, row_send, got_recv,
):
    rows = x_ref.shape[0]
    reach, _, wide = s_ref.shape
    dim = kv_ref.shape[2] // 2
    my = lax.axis_index("seq")
    my_head = lax.axis_index("head")
    grid_rows = lax.axis_size("seq") // 8
    row = my // 8
    chip = my // 2 - row * 4
    core = my - (my // 2) * 2
    order = my // 2

    def place(r, x, c):
        return (r * 8 + x * 2 + c, my_head)

    def remote(source, target, send, recv, device):
        return pltpu.make_async_remote_copy(
            src_ref=source,
            dst_ref=target,
            send_sem=send,
            recv_sem=recv,
            device_id=device,
            device_id_type=pl.DeviceIdType.MESH,
        )

    def slot_copy(source, target, send, device):
        return remote(kv_ref.at[source], kv_ref.at[target], send, slot_recv.at[target], device)

    def arrived(slot):
        slot_copy(slot, slot, chip_send.at[0], place(row, chip, core)).wait_recv()

    def got(index):
        remote(
            got_ref.at[index],
            got_ref.at[index],
            row_send.at[0],
            got_recv.at[index],
            place(row, chip, core),
        ).wait_recv()

    extra = 13
    has_next = row < grid_rows - 1
    relays = chip >= 3 - core

    def to_next(act):
        @pl.when(has_next)
        def _():
            act(slot_copy(0, 8, across_send.at[0], place(row + 1, chip, core)))

    def to_second(act):
        @pl.when((row >= 1) & has_next & relays)
        def _():
            act(slot_copy(8, extra, across_send.at[1], place(row + 1, chip, core)))

    def along_own(act):
        for other in range(4):
            @pl.when(chip < other)
            def _(other=other):
                act(
                    slot_copy(
                        0, 2 * (other - chip), chip_send.at[other], place(row, other, core)
                    )
                )

    def along_first(act):
        for other in range(4):
            @pl.when((row >= 1) & (chip != other) & (chip + 1 + core >= other))
            def _(other=other):
                act(
                    slot_copy(
                        8, 8 + 2 * (other - chip), chip_send.at[4 + other], place(row, other, core)
                    )
                )

    def along_second(act):
        for other in range(2):
            @pl.when((row >= 2) & (chip - 3 + core >= other))
            def _(other=other):
                act(
                    slot_copy(
                        extra,
                        16 + 2 * (other - chip),
                        chip_send.at[8 + other],
                        place(row, other, core),
                    )
                )

    def to_partner(j, act):
        @pl.when(core == 0)
        def _():
            act(slot_copy(2 * j, 2 * j + 1, partner_send.at[j], place(row, chip, 1)))

        @pl.when((core == 1) & (j >= 1))
        def _():
            act(slot_copy(2 * j, 2 * j - 1, partner_send.at[j], place(row, chip, 0)))

    def start(copy):
        copy.start()

    def sent(copy):
        copy.wait_send()

    kv_ref[0] = x_ref[:, 4 * dim :]

    barrier = pltpu.get_barrier_semaphore()

    def greet(device):
        pl.semaphore_signal(
            barrier, inc=1, device_id=device, device_id_type=pl.DeviceIdType.MESH
        )

    for step in range(1, 4):
        greet(place(row, (chip + step) % 4, core))
    greet(place(row, chip, 1 - core))

    greet(place((row + 1) % grid_rows, chip, core))
    greet(place((row + grid_rows - 1) % grid_rows, chip, core))
    pl.semaphore_wait(barrier, 6)

    to_next(start)
    along_own(start)
    to_partner(0, start)

    q = jnp.concatenate([x_ref[:, :dim], x_ref[:, dim : 2 * dim]], axis=0)
    g = jnp.concatenate([x_ref[:, 2 * dim : 3 * dim], x_ref[:, 3 * dim : 4 * dim]], axis=0)
    lo = lo_ref[...]
    pos = pos_ref[...]

    def scores(d, top):
        contract = (((1,), (1,)), ((), ()))
        s = lax.dot_general(kv_ref[d, :, :dim], q, contract, preferred_element_type=jnp.float32)
        dp_ref[d] = lax.dot_general(
            kv_ref[d, :, dim:], g, contract, preferred_element_type=jnp.float32
        )
        k_pos = (my - d) * rows + lax.broadcasted_iota(jnp.int32, (rows, wide), 0)
        s = jnp.where((k_pos >= lo) & (k_pos <= pos), s, masked_value)
        s_ref[d] = s
        return jnp.maximum(top, jnp.max(s, axis=0, keepdims=True))

    top = scores(0, jnp.full((1, wide), masked_value, jnp.float32))

    @pl.when(row >= 1)
    def _():
        arrived(8)

    to_second(start)
    along_first(start)

    def even_step(j, top):
        @pl.when(j != 4)
        def _():
            arrived(2 * j)

        to_partner(j, start)
        return scores(2 * j, top)

    even_end = jnp.minimum(order, 5) + 1
    top = lax.fori_loop(1, jnp.minimum(even_end, 3), even_step, top)

    @pl.when((row >= 2) & relays)
    def _():
        arrived(extra)

    along_second(start)
    top = lax.fori_loop(3, even_end, even_step, top)
    last = (core == 1) & (order >= 6)

    @pl.when(last)
    def _():
        arrived(12)
        slot_copy(12, 11, partner_send.at[6], place(row, chip, 0)).start()

    def odd_step(j, top):
        arrived(2 * j + 1)
        return scores(2 * j + 1, top)

    top = lax.fori_loop(0, jnp.minimum(order + core, 6), odd_step, top)
    top = top * exp2_scale

    def second(d, state):
        total, delta = state
        p = jnp.exp2(s_ref[d] * exp2_scale - top)
        s_ref[d] = p
        return (
            total + jnp.sum(p, axis=0, keepdims=True),
            delta + jnp.sum(p * dp_ref[d], axis=0, keepdims=True),
        )

    zero = jnp.zeros((1, wide), jnp.float32)
    total, delta = lax.fori_loop(0, jnp.minimum(my + 1, reach), second, (zero, zero))
    inverse = 1.0 / total
    delta = delta * inverse
    column = jnp.transpose(jnp.broadcast_to(inverse, (dim, wide)))
    g_low = (g.astype(jnp.float32) * column).astype(jnp.bfloat16)
    q_low = (q.astype(jnp.float32) * (column * score_scale)).astype(jnp.bfloat16)
    dq_ref[...] = jnp.zeros_like(dq_ref)

    def gradients(d):
        p = s_ref[d]
        ds = (p * (dp_ref[d] - delta)).astype(jnp.bfloat16)
        dv = jnp.dot(p.astype(jnp.bfloat16), g_low, preferred_element_type=jnp.float32)
        dk = jnp.dot(ds, q_low, preferred_element_type=jnp.float32)
        dq_ref[...] += lax.dot_general(
            kv_ref[d, :, :dim], ds, (((0,), (0,)), ((), ())), preferred_element_type=jnp.float32
        )
        return dk, dv

    def odd_copy(j):
        return remote(
            odd_ref.at[j],
            pair_ref.at[j],
            odd_send.at[j],
            pair_recv.at[j],
            place(row, chip, 1 - core),
        )

    def dispatch(k, act):
        @pl.when((k >= 1) & (k <= chip))
        def _():
            act(
                remote(
                    even_ref.at[k],
                    got_ref.at[k],
                    even_send.at[k],
                    got_recv.at[k],
                    place(row, chip - k, core),
                )
            )

        @pl.when((k > chip) & (k <= chip + 4) & (k != 4))
        def _():
            act(
                remote(
                    even_ref.at[k],
                    got_ref.at[4 + chip],
                    even_send.at[k],
                    got_recv.at[4 + chip],
                    place(row, chip - k + 4, core),
                )
            )

        @pl.when(k > chip + 4)
        def _():
            act(
                remote(
                    even_ref.at[k],
                    got_ref.at[8 + chip],
                    even_send.at[k],
                    got_recv.at[8 + chip],
                    place(row, chip - k + 8, core),
                )
            )

    def third(i, carry):
        j = jnp.minimum(order, 5) - i
        sends = (core == 1) | (j < order)
        gets = (core == 0) | (j < order)

        @pl.when(sends)
        def _():
            dk, dv = gradients(2 * j + 1)
            odd_ref[j, :, :dim] = dk.astype(jnp.bfloat16)
            odd_ref[j, :, dim:] = dv.astype(jnp.bfloat16)
            odd_copy(j).start()

        @pl.when(gets & (j + core <= 5))
        def _():
            dk, dv = gradients(2 * (j + core))
            odd_copy(j).wait_recv()
            even_ref[j + core, :, :dim] = (
                dk + pair_ref[j, :, :dim].astype(jnp.float32)
            ).astype(jnp.bfloat16)
            even_ref[j + core, :, dim:] = (
                dv + pair_ref[j, :, dim:].astype(jnp.float32)
            ).astype(jnp.bfloat16)
            dispatch(j + core, start)

        @pl.when(gets & (j + core == 6))
        def _():
            odd_copy(j).wait_recv()
            even_ref[6] = pair_ref[j]
            dispatch(6, start)

        return carry

    lax.fori_loop(0, jnp.minimum(order, 5) + 1, third, 0)

    @pl.when(core == 1)
    def _():
        dk, dv = gradients(0)
        even_ref[0, :, :dim] = dk.astype(jnp.bfloat16)
        even_ref[0, :, dim:] = dv.astype(jnp.bfloat16)

    dq = jnp.transpose(dq_ref[...] * (inverse * score_scale)).astype(jnp.bfloat16)
    out_ref[:, :dim] = dq[:rows]
    out_ref[:, dim : 2 * dim] = dq[rows:]

    acc = dp_ref.at[0, :, : 2 * dim]

    def add(index):
        got(index)
        acc[...] += got_ref[index].astype(jnp.float32)

    def row_copy(index):
        return remote(
            row_ref.at[index],
            got_ref.at[10 + index],
            row_send.at[index],
            got_recv.at[10 + index],
            place(row - 1, chip, core),
        )

    @pl.when((row >= 2) & relays)
    def _():
        acc[...] = jnp.zeros((rows, 2 * dim), jnp.float32)
        for other in range(2):
            @pl.when(chip - 3 + core >= other)
            def _(other=other):
                add(8 + other)

        row_ref[1] = acc[...].astype(jnp.bfloat16)
        row_copy(1).start()

    @pl.when(row >= 1)
    def _():
        acc[...] = even_ref[4].astype(jnp.float32)
        for other in range(4):
            @pl.when((chip != other) & (chip + 1 + core >= other))
            def _(other=other):
                add(4 + other)

        @pl.when(has_next & relays)
        def _():
            add(11)

        row_ref[0] = acc[...].astype(jnp.bfloat16)
        row_copy(0).start()

    acc[...] = even_ref[0].astype(jnp.float32)
    for k in range(1, 4):
        @pl.when(chip + k <= 3)
        def _(k=k):
            add(k)

    @pl.when(has_next)
    def _():
        add(10)

    out_ref[:, 2 * dim :] = acc[...].astype(jnp.bfloat16)

    to_next(sent)
    along_own(sent)
    to_second(sent)
    along_first(sent)
    along_second(sent)

    def sent_pair(j, carry):
        to_partner(j, sent)
        return carry

    lax.fori_loop(0, even_end, sent_pair, 0)

    @pl.when(last)
    def _():
        slot_copy(12, 11, partner_send.at[6], place(row, chip, 0)).wait_send()

    def sent_gradients(j, carry):
        @pl.when((core == 1) | (j < order))
        def _():
            odd_copy(j).wait_send()

        @pl.when((core == 0) | (j < order))
        def _():
            dispatch(j + core, sent)

        return carry

    lax.fori_loop(0, even_end, sent_gradients, 0)

    @pl.when((row >= 2) & relays)
    def _():
        row_copy(1).wait_send()

    @pl.when(row >= 1)
    def _():
        row_copy(0).wait_send()


def body(queries, keys, values, output_gradient, doc_lengths):
    chunk, kv_heads, dim = keys.shape
    group = queries.shape[1] // kv_heads
    seq_count = lax.axis_size("seq")
    my_index = lax.axis_index("seq")
    packed = jnp.concatenate(
        [
            queries.reshape(chunk, kv_heads, group * dim),
            output_gradient.reshape(chunk, kv_heads, group * dim),
            keys,
            values,
        ],
        axis=2,
    )
    local = lax.all_to_all(packed, "head", split_axis=1, concat_axis=0, tiled=True)
    rows = local.shape[0]
    local = local.reshape(rows, local.shape[2])
    reach = (WINDOW - 1) // rows + 2
    pos = my_index * rows + jnp.arange(rows, dtype=jnp.int32)
    ends = jnp.cumsum(doc_lengths)
    doc_start = jnp.max(jnp.where(ends[None, :] <= pos[:, None], ends[None, :], 0), axis=1)
    lo = jnp.maximum(doc_start, pos - (WINDOW - 1))
    wide = group * rows
    lo = jnp.tile(lo, group).reshape(1, wide).astype(jnp.int32)
    pos = jnp.tile(pos, group).reshape(1, wide)
    vmem = pl.BlockSpec(memory_space=pltpu.VMEM)
    block = (rows, 2 * dim)
    dma = pltpu.SemaphoreType.DMA
    back = pl.pallas_call(
        attention_kernel,
        out_shape=jax.ShapeDtypeStruct((rows, (group + 2) * dim), jnp.bfloat16),
        in_specs=[vmem, vmem, vmem],
        out_specs=vmem,
        scratch_shapes=[
            pltpu.VMEM((14,) + block, jnp.bfloat16),
            pltpu.VMEM((reach, rows, wide), jnp.float32),
            pltpu.VMEM((reach, rows, wide), jnp.float32),
            pltpu.VMEM((dim, wide), jnp.float32),
            pltpu.VMEM((6,) + block, jnp.bfloat16),
            pltpu.VMEM((7,) + block, jnp.bfloat16),
            pltpu.VMEM((6,) + block, jnp.bfloat16),
            pltpu.VMEM((12,) + block, jnp.bfloat16),
            pltpu.VMEM((2,) + block, jnp.bfloat16),
            dma((7,)),
            dma((2,)),
            dma((10,)),
            dma((14,)),
            dma((6,)),
            dma((7,)),
            dma((6,)),
            dma((2,)),
            dma((12,)),
        ],
        compiler_params=pltpu.CompilerParams(
            vmem_limit_bytes=60 * 2**20, collective_id=0, has_side_effects=True
        ),
        name="attention_backward",
    )(lo, pos, local)
    back = back.reshape(rows, 1, (group + 2) * dim)
    back = lax.all_to_all(back, "head", split_axis=0, concat_axis=1, tiled=True)
    return (
        back[:, :, : group * dim].reshape(queries.shape),
        back[:, :, group * dim : (group + 1) * dim],
        back[:, :, (group + 1) * dim :],
    )


def solution(mesh):
    spec = P(("seq", "head"), None, None)
    return jax.shard_map(
        body,
        mesh=mesh,
        in_specs=(spec, spec, spec, spec, P()),
        out_specs=(spec, spec, spec),
        check_vma=False,
    )
```

```python
import math

import jax
import jax.numpy as jnp
from jax import lax
from jax.experimental import pallas as pl
from jax.experimental.pallas import tpu as pltpu
from jax.sharding import PartitionSpec as P

WINDOW = 4096

score_scale = 144.0 ** (-0.5)
exp2_scale = score_scale * math.log2(math.e)
masked_value = -1e30


def attention_kernel(
    lengths_ref, kv_out_ref, qg_out_ref, dq_back_ref, dkv_back_ref,
    kv_in_ref, qg_in_ref, dq_out_ref, dkv_out_ref, kv_ref, s_ref, dp_ref, dq_ref, odd_ref, even_ref, pair_ref, got_ref, row_ref,
    partner_send, across_send, chip_send, slot_recv, odd_send, even_send, pair_recv, row_send, got_recv,
    swap_send, swap_recv,
):
    heads, chunk, _ = kv_out_ref.shape
    rows = heads * chunk
    reach, _, wide = s_ref.shape
    dim = kv_ref.shape[2] // 2
    my = lax.axis_index("seq")
    my_head = lax.axis_index("head")
    grid_rows = lax.axis_size("seq") // 8
    row = my // 8
    chip = my // 2 - row * 4
    core = my - (my // 2) * 2
    order = my // 2

    def place(r, x, c):
        return (r * 8 + x * 2 + c, my_head)

    def remote(source, target, send, recv, device):
        return pltpu.make_async_remote_copy(
            src_ref=source,
            dst_ref=target,
            send_sem=send,
            recv_sem=recv,
            device_id=device,
            device_id_type=pl.DeviceIdType.MESH,
        )

    def slot_copy(source, target, send, device):
        return remote(kv_ref.at[source], kv_ref.at[target], send, slot_recv.at[target], device)

    def arrived(slot):
        slot_copy(slot, slot, chip_send.at[0], place(row, chip, core)).wait_recv()

    def got(index):
        remote(
            got_ref.at[index],
            got_ref.at[index],
            row_send.at[0],
            got_recv.at[index],
            place(row, chip, core),
        ).wait_recv()

    extra = 13
    has_next = row < grid_rows - 1
    relays = chip >= 3 - core

    def to_next(act):
        @pl.when(has_next)
        def _():
            act(slot_copy(0, 8, across_send.at[0], place(row + 1, chip, core)))

    def to_second(act):
        @pl.when((row >= 1) & has_next & relays)
        def _():
            act(slot_copy(8, extra, across_send.at[1], place(row + 1, chip, core)))

    def along_own(act):
        for other in range(4):
            @pl.when(chip < other)
            def _(other=other):
                act(
                    slot_copy(
                        0, 2 * (other - chip), chip_send.at[other], place(row, other, core)
                    )
                )

    def along_first(act):
        for other in range(4):
            @pl.when((row >= 1) & (chip != other) & (chip + 1 + core >= other))
            def _(other=other):
                act(
                    slot_copy(
                        8, 8 + 2 * (other - chip), chip_send.at[4 + other], place(row, other, core)
                    )
                )

    def along_second(act):
        for other in range(2):
            @pl.when((row >= 2) & (chip - 3 + core >= other))
            def _(other=other):
                act(
                    slot_copy(
                        extra,
                        16 + 2 * (other - chip),
                        chip_send.at[8 + other],
                        place(row, other, core),
                    )
                )

    def to_partner(j, act):
        @pl.when(core == 0)
        def _():
            act(slot_copy(2 * j, 2 * j + 1, partner_send.at[j], place(row, chip, 1)))

        @pl.when((core == 1) & (j >= 1))
        def _():
            act(slot_copy(2 * j, 2 * j - 1, partner_send.at[j], place(row, chip, 0)))

    def start(copy):
        copy.start()

    def sent(copy):
        copy.wait_send()

    def swap(n, source, target, peer):
        return remote(
            source.at[peer],
            target.at[my_head],
            swap_send.at[n * heads + peer],
            swap_recv.at[n * heads + my_head],
            (my, peer),
        )

    def swap_start(n, source, target):
        def one(step, carry):
            swap(n, source, target, (my_head + step) % heads).start()
            return carry

        lax.fori_loop(1, heads, one, 0)
        target[my_head] = source[my_head]

    def swap_arrived(n, source, target):
        def one(step, carry):
            peer = (my_head + step) % heads
            remote(
                source.at[peer],
                target.at[peer],
                swap_send.at[n * heads + peer],
                swap_recv.at[n * heads + peer],
                (my, peer),
            ).wait_recv()
            return carry

        lax.fori_loop(1, heads, one, 0)

    def swap_sent(n, source, target):
        def one(step, carry):
            swap(n, source, target, (my_head + step) % heads).wait_send()
            return carry

        lax.fori_loop(1, heads, one, 0)

    barrier = pltpu.get_barrier_semaphore()

    def greet(device):
        pl.semaphore_signal(
            barrier, inc=1, device_id=device, device_id_type=pl.DeviceIdType.MESH
        )

    for step in range(1, 4):
        greet(place(row, (chip + step) % 4, core))
    greet(place(row, chip, 1 - core))

    greet(place((row + 1) % grid_rows, chip, core))
    greet(place((row + grid_rows - 1) % grid_rows, chip, core))

    def greet_head(step, carry):
        greet((my, (my_head + step) % heads))
        return carry

    lax.fori_loop(1, heads, greet_head, 0)
    pl.semaphore_wait(barrier, 5 + heads)
    swap_start(0, kv_out_ref, kv_in_ref)
    swap_start(1, qg_out_ref, qg_in_ref)
    swap_arrived(0, kv_out_ref, kv_in_ref)
    kv_ref[0] = kv_in_ref[...].astype(jnp.float32).reshape(rows, 2 * dim).astype(jnp.bfloat16)

    to_next(start)
    along_own(start)
    to_partner(0, start)

    pos = my * rows + lax.broadcasted_iota(jnp.int32, (1, rows), 1)
    end = lengths_ref[0]
    lo = jnp.zeros((1, rows), jnp.int32)
    for document in range(1, lengths_ref.shape[0]):
        lo = jnp.where(pos >= end, end, lo)
        end = end + lengths_ref[document]
    lo = jnp.maximum(lo, pos - (WINDOW - 1))
    pos = jnp.concatenate([pos] * (wide // rows), axis=1)
    lo = jnp.concatenate([lo] * (wide // rows), axis=1)
    swap_arrived(1, qg_out_ref, qg_in_ref)
    qg = qg_in_ref[...].astype(jnp.float32).reshape(rows, 4 * dim).astype(jnp.bfloat16)
    q = jnp.concatenate([qg[:, :dim], qg[:, dim : 2 * dim]], axis=0)
    g = jnp.concatenate([qg[:, 2 * dim : 3 * dim], qg[:, 3 * dim :]], axis=0)

    def scores(d, top):
        contract = (((1,), (1,)), ((), ()))
        s = lax.dot_general(kv_ref[d, :, :dim], q, contract, preferred_element_type=jnp.float32)
        dp_ref[d] = lax.dot_general(
            kv_ref[d, :, dim:], g, contract, preferred_element_type=jnp.float32
        )
        k_pos = (my - d) * rows + lax.broadcasted_iota(jnp.int32, (rows, wide), 0)
        s = jnp.where((k_pos >= lo) & (k_pos <= pos), s, masked_value)
        s_ref[d] = s
        return jnp.maximum(top, jnp.max(s, axis=0, keepdims=True))

    top = scores(0, jnp.full((1, wide), masked_value, jnp.float32))

    @pl.when(row >= 1)
    def _():
        arrived(8)

    to_second(start)
    along_first(start)

    def even_step(j, top):
        @pl.when(j != 4)
        def _():
            arrived(2 * j)

        to_partner(j, start)
        return scores(2 * j, top)

    even_end = jnp.minimum(order, 5) + 1
    top = lax.fori_loop(1, jnp.minimum(even_end, 3), even_step, top)

    @pl.when((row >= 2) & relays)
    def _():
        arrived(extra)

    along_second(start)
    top = lax.fori_loop(3, even_end, even_step, top)
    last = (core == 1) & (order >= 6)

    @pl.when(last)
    def _():
        arrived(12)
        slot_copy(12, 11, partner_send.at[6], place(row, chip, 0)).start()

    def odd_step(j, top):
        arrived(2 * j + 1)
        return scores(2 * j + 1, top)

    top = lax.fori_loop(0, jnp.minimum(order + core, 6), odd_step, top)
    top = top * exp2_scale

    def second(d, state):
        total, delta = state
        p = jnp.exp2(s_ref[d] * exp2_scale - top)
        s_ref[d] = p
        return (
            total + jnp.sum(p, axis=0, keepdims=True),
            delta + jnp.sum(p * dp_ref[d], axis=0, keepdims=True),
        )

    zero = jnp.zeros((1, wide), jnp.float32)
    total, delta = lax.fori_loop(0, jnp.minimum(my + 1, reach), second, (zero, zero))
    inverse = 1.0 / total
    delta = delta * inverse
    column = jnp.transpose(jnp.broadcast_to(inverse, (dim, wide)))
    g_low = (g.astype(jnp.float32) * column).astype(jnp.bfloat16)
    q_low = (q.astype(jnp.float32) * (column * score_scale)).astype(jnp.bfloat16)
    dq_ref[...] = jnp.zeros_like(dq_ref)

    def gradients(d):
        p = s_ref[d]
        ds = (p * (dp_ref[d] - delta)).astype(jnp.bfloat16)
        dv = jnp.dot(p.astype(jnp.bfloat16), g_low, preferred_element_type=jnp.float32)
        dk = jnp.dot(ds, q_low, preferred_element_type=jnp.float32)
        dq_ref[...] += lax.dot_general(
            kv_ref[d, :, :dim], ds, (((0,), (0,)), ((), ())), preferred_element_type=jnp.float32
        )
        return dk, dv

    def odd_copy(j):
        return remote(
            odd_ref.at[j],
            pair_ref.at[j],
            odd_send.at[j],
            pair_recv.at[j],
            place(row, chip, 1 - core),
        )

    def dispatch(k, act):
        @pl.when((k >= 1) & (k <= chip))
        def _():
            act(
                remote(
                    even_ref.at[k],
                    got_ref.at[k],
                    even_send.at[k],
                    got_recv.at[k],
                    place(row, chip - k, core),
                )
            )

        @pl.when((k > chip) & (k <= chip + 4) & (k != 4))
        def _():
            act(
                remote(
                    even_ref.at[k],
                    got_ref.at[4 + chip],
                    even_send.at[k],
                    got_recv.at[4 + chip],
                    place(row, chip - k + 4, core),
                )
            )

        @pl.when(k > chip + 4)
        def _():
            act(
                remote(
                    even_ref.at[k],
                    got_ref.at[8 + chip],
                    even_send.at[k],
                    got_recv.at[8 + chip],
                    place(row, chip - k + 8, core),
                )
            )

    def third(i, carry):
        j = jnp.minimum(order, 5) - i
        sends = (core == 1) | (j < order)
        gets = (core == 0) | (j < order)

        @pl.when(sends)
        def _():
            dk, dv = gradients(2 * j + 1)
            odd_ref[j, :, :dim] = dk.astype(jnp.bfloat16)
            odd_ref[j, :, dim:] = dv.astype(jnp.bfloat16)
            odd_copy(j).start()

        @pl.when(gets & (j + core <= 5))
        def _():
            dk, dv = gradients(2 * (j + core))
            odd_copy(j).wait_recv()
            even_ref[j + core, :, :dim] = (
                dk + pair_ref[j, :, :dim].astype(jnp.float32)
            ).astype(jnp.bfloat16)
            even_ref[j + core, :, dim:] = (
                dv + pair_ref[j, :, dim:].astype(jnp.float32)
            ).astype(jnp.bfloat16)
            dispatch(j + core, start)

        @pl.when(gets & (j + core == 6))
        def _():
            odd_copy(j).wait_recv()
            even_ref[6] = pair_ref[j]
            dispatch(6, start)

        return carry

    lax.fori_loop(0, jnp.minimum(order, 5) + 1, third, 0)

    @pl.when(core == 1)
    def _():
        dk, dv = gradients(0)
        even_ref[0, :, :dim] = dk.astype(jnp.bfloat16)
        even_ref[0, :, dim:] = dv.astype(jnp.bfloat16)

    dq = jnp.transpose(dq_ref[...] * (inverse * score_scale))
    for part in range(2):
        dq_out_ref[:, :, part * dim : (part + 1) * dim] = (
            dq[part * rows : (part + 1) * rows].reshape(heads, chunk, dim).astype(jnp.bfloat16)
        )
    swap_start(2, dq_out_ref, dq_back_ref)

    acc = dp_ref.at[0, :, : 2 * dim]

    def add(index):
        got(index)
        acc[...] += got_ref[index].astype(jnp.float32)

    def row_copy(index):
        return remote(
            row_ref.at[index],
            got_ref.at[10 + index],
            row_send.at[index],
            got_recv.at[10 + index],
            place(row - 1, chip, core),
        )

    @pl.when((row >= 2) & relays)
    def _():
        acc[...] = jnp.zeros((rows, 2 * dim), jnp.float32)
        for other in range(2):
            @pl.when(chip - 3 + core >= other)
            def _(other=other):
                add(8 + other)

        row_ref[1] = acc[...].astype(jnp.bfloat16)
        row_copy(1).start()

    @pl.when(row >= 1)
    def _():
        acc[...] = even_ref[4].astype(jnp.float32)
        for other in range(4):
            @pl.when((chip != other) & (chip + 1 + core >= other))
            def _(other=other):
                add(4 + other)

        @pl.when(has_next & relays)
        def _():
            add(11)

        row_ref[0] = acc[...].astype(jnp.bfloat16)
        row_copy(0).start()

    acc[...] = even_ref[0].astype(jnp.float32)
    for k in range(1, 4):
        @pl.when(chip + k <= 3)
        def _(k=k):
            add(k)

    @pl.when(has_next)
    def _():
        add(10)

    dkv_out_ref[...] = acc[...].reshape(heads, chunk, 2 * dim).astype(jnp.bfloat16)
    swap_start(3, dkv_out_ref, dkv_back_ref)

    to_next(sent)
    along_own(sent)
    to_second(sent)
    along_first(sent)
    along_second(sent)

    def sent_pair(j, carry):
        to_partner(j, sent)
        return carry

    lax.fori_loop(0, even_end, sent_pair, 0)

    @pl.when(last)
    def _():
        slot_copy(12, 11, partner_send.at[6], place(row, chip, 0)).wait_send()

    def sent_gradients(j, carry):
        @pl.when((core == 1) | (j < order))
        def _():
            odd_copy(j).wait_send()

        @pl.when((core == 0) | (j < order))
        def _():
            dispatch(j + core, sent)

        return carry

    lax.fori_loop(0, even_end, sent_gradients, 0)

    @pl.when((row >= 2) & relays)
    def _():
        row_copy(1).wait_send()

    @pl.when(row >= 1)
    def _():
        row_copy(0).wait_send()

    swap_sent(0, kv_out_ref, kv_in_ref)
    swap_sent(1, qg_out_ref, qg_in_ref)
    swap_sent(2, dq_out_ref, dq_back_ref)
    swap_sent(3, dkv_out_ref, dkv_back_ref)
    swap_arrived(2, dq_out_ref, dq_back_ref)
    swap_arrived(3, dkv_out_ref, dkv_back_ref)


def body(queries, keys, values, output_gradient, doc_lengths):
    chunk, kv_heads, dim = keys.shape
    group = queries.shape[1] // kv_heads
    rows = chunk * lax.axis_size("head")
    by_head = lambda parts: jnp.transpose(
        jnp.concatenate([part.reshape(chunk, kv_heads, -1) for part in parts], axis=2), (1, 0, 2)
    )
    kv = by_head([keys, values])
    qg = by_head([queries, output_gradient])
    reach = (WINDOW - 1) // rows + 2
    wide = group * rows
    vmem = pl.BlockSpec(memory_space=pltpu.VMEM)
    block = (rows, 2 * dim)
    swapped = (kv_heads, chunk, 2 * dim)
    low = jnp.bfloat16
    dma = pltpu.SemaphoreType.DMA
    dq, dkv = pl.pallas_call(
        attention_kernel,
        out_shape=(
            jax.ShapeDtypeStruct(swapped, low),
            jax.ShapeDtypeStruct(swapped, low),
        ),
        in_specs=[pl.BlockSpec(memory_space=pltpu.SMEM), vmem, vmem],
        out_specs=(vmem, vmem),
        scratch_shapes=[
            pltpu.VMEM(swapped, low),
            pltpu.VMEM((kv_heads, chunk, 4 * dim), low),
            pltpu.VMEM(swapped, low),
            pltpu.VMEM(swapped, low),
            pltpu.VMEM((14,) + block, low),
            pltpu.VMEM((reach, rows, wide), jnp.float32),
            pltpu.VMEM((reach, rows, wide), jnp.float32),
            pltpu.VMEM((dim, wide), jnp.float32),
            pltpu.VMEM((6,) + block, low),
            pltpu.VMEM((7,) + block, low),
            pltpu.VMEM((6,) + block, low),
            pltpu.VMEM((12,) + block, low),
            pltpu.VMEM((2,) + block, low),
            dma((7,)),
            dma((2,)),
            dma((10,)),
            dma((14,)),
            dma((6,)),
            dma((7,)),
            dma((6,)),
            dma((2,)),
            dma((12,)),
            dma((4 * kv_heads,)),
            dma((4 * kv_heads,)),
        ],
        compiler_params=pltpu.CompilerParams(
            vmem_limit_bytes=60 * 2**20, collective_id=0, has_side_effects=True
        ),
        name="attention_backward",
    )(doc_lengths, kv, qg)
    by_token = lambda part: jnp.transpose(part, (1, 0, 2))
    return (
        by_token(dq).reshape(queries.shape),
        by_token(dkv[:, :, :dim]),
        by_token(dkv[:, :, dim:]),
    )


def solution(mesh):
    spec = P(("seq", "head"), None, None)
    return jax.shard_map(
        body,
        mesh=mesh,
        in_specs=(spec, spec, spec, spec, P()),
        out_specs=(spec, spec, spec),
        check_vma=False,
    )
```

```python
import math

import jax
import jax.numpy as jnp
from jax import lax
from jax.experimental import pallas as pl
from jax.experimental.pallas import tpu as pltpu
from jax.sharding import PartitionSpec as P

WINDOW = 4096

score_scale = 144.0 ** (-0.5)
exp2_scale = score_scale * math.log2(math.e)
masked_value = -1e30


def attention_kernel(
    lengths_ref, kv_out_ref, qg_out_ref, dq_back_ref, dkv_back_ref,
    kv_in_ref, qg_in_ref, dq_out_ref, dkv_out_ref, kv_ref, s_ref, dp_ref, top_ref, sum_ref, dq_ref, odd_ref, even_ref, pair_ref, got_ref, row_ref,
    partner_send, across_send, chip_send, slot_recv, odd_send, even_send, pair_recv, row_send, got_recv,
    swap_send, swap_recv,
):
    heads, chunk, _ = kv_out_ref.shape
    rows = heads * chunk
    reach, _, wide = s_ref.shape
    dim = kv_ref.shape[2] // 2
    my = lax.axis_index("seq")
    my_head = lax.axis_index("head")
    grid_rows = lax.axis_size("seq") // 8
    row = my // 8
    chip = my // 2 - row * 4
    core = my - (my // 2) * 2
    order = my // 2

    def place(r, x, c):
        return (r * 8 + x * 2 + c, my_head)

    def remote(source, target, send, recv, device):
        return pltpu.make_async_remote_copy(
            src_ref=source,
            dst_ref=target,
            send_sem=send,
            recv_sem=recv,
            device_id=device,
            device_id_type=pl.DeviceIdType.MESH,
        )

    def slot_copy(source, target, send, device):
        return remote(kv_ref.at[source], kv_ref.at[target], send, slot_recv.at[target], device)

    def arrived(slot):
        slot_copy(slot, slot, chip_send.at[0], place(row, chip, core)).wait_recv()

    def got(index):
        remote(
            got_ref.at[index],
            got_ref.at[index],
            row_send.at[0],
            got_recv.at[index],
            place(row, chip, core),
        ).wait_recv()

    extra = 13
    has_next = row < grid_rows - 1
    relays = chip >= 3 - core

    def to_next(act):
        @pl.when(has_next)
        def _():
            act(slot_copy(0, 8, across_send.at[0], place(row + 1, chip, core)))

    def to_second(act):
        @pl.when((row >= 1) & has_next & relays)
        def _():
            act(slot_copy(8, extra, across_send.at[1], place(row + 1, chip, core)))

    def along_own(act):
        for other in range(4):
            @pl.when(chip < other)
            def _(other=other):
                act(
                    slot_copy(
                        0, 2 * (other - chip), chip_send.at[other], place(row, other, core)
                    )
                )

    def along_first(act):
        for other in range(4):
            @pl.when((row >= 1) & (chip != other) & (chip + 1 + core >= other))
            def _(other=other):
                act(
                    slot_copy(
                        8, 8 + 2 * (other - chip), chip_send.at[4 + other], place(row, other, core)
                    )
                )

    def along_second(act):
        for other in range(2):
            @pl.when((row >= 2) & (chip - 3 + core >= other))
            def _(other=other):
                act(
                    slot_copy(
                        extra,
                        16 + 2 * (other - chip),
                        chip_send.at[8 + other],
                        place(row, other, core),
                    )
                )

    def to_partner(j, act):
        @pl.when(core == 0)
        def _():
            act(slot_copy(2 * j, 2 * j + 1, partner_send.at[j], place(row, chip, 1)))

        @pl.when((core == 1) & (j >= 1))
        def _():
            act(slot_copy(2 * j, 2 * j - 1, partner_send.at[j], place(row, chip, 0)))

    def start(copy):
        copy.start()

    def sent(copy):
        copy.wait_send()

    def swap(n, source, target, peer):
        return remote(
            source.at[peer],
            target.at[my_head],
            swap_send.at[n * heads + peer],
            swap_recv.at[n * heads + my_head],
            (my, peer),
        )

    def swap_start(n, source, target):
        def one(step, carry):
            swap(n, source, target, (my_head + step) % heads).start()
            return carry

        lax.fori_loop(1, heads, one, 0)
        target[my_head] = source[my_head]

    def swap_arrived(n, source, target):
        def one(step, carry):
            peer = (my_head + step) % heads
            remote(
                source.at[peer],
                target.at[peer],
                swap_send.at[n * heads + peer],
                swap_recv.at[n * heads + peer],
                (my, peer),
            ).wait_recv()
            return carry

        lax.fori_loop(1, heads, one, 0)

    def swap_sent(n, source, target):
        def one(step, carry):
            swap(n, source, target, (my_head + step) % heads).wait_send()
            return carry

        lax.fori_loop(1, heads, one, 0)

    barrier = pltpu.get_barrier_semaphore()

    def greet(device):
        pl.semaphore_signal(
            barrier, inc=1, device_id=device, device_id_type=pl.DeviceIdType.MESH
        )

    for step in range(1, 4):
        greet(place(row, (chip + step) % 4, core))
    greet(place(row, chip, 1 - core))

    greet(place((row + 1) % grid_rows, chip, core))
    greet(place((row + grid_rows - 1) % grid_rows, chip, core))

    def greet_head(step, carry):
        greet((my, (my_head + step) % heads))
        return carry

    lax.fori_loop(1, heads, greet_head, 0)
    pl.semaphore_wait(barrier, 5 + heads)
    swap_start(0, kv_out_ref, kv_in_ref)
    swap_arrived(0, kv_out_ref, kv_in_ref)
    kv_ref[0] = kv_in_ref[...].astype(jnp.float32).reshape(rows, 2 * dim).astype(jnp.bfloat16)

    to_next(start)
    along_own(start)
    to_partner(0, start)
    swap_start(1, qg_out_ref, qg_in_ref)

    pos = my * rows + lax.broadcasted_iota(jnp.int32, (1, rows), 1)
    end = lengths_ref[0]
    lo = jnp.zeros((1, rows), jnp.int32)
    for document in range(1, lengths_ref.shape[0]):
        lo = jnp.where(pos >= end, end, lo)
        end = end + lengths_ref[document]
    lo = jnp.maximum(lo, pos - (WINDOW - 1))
    pos = jnp.concatenate([pos] * (wide // rows), axis=1)
    lo = jnp.concatenate([lo] * (wide // rows), axis=1)
    swap_arrived(1, qg_out_ref, qg_in_ref)
    qg = qg_in_ref[...].astype(jnp.float32).reshape(rows, 4 * dim).astype(jnp.bfloat16)
    q = jnp.concatenate([qg[:, :dim], qg[:, dim : 2 * dim]], axis=0)
    g = jnp.concatenate([qg[:, 2 * dim : 3 * dim], qg[:, 3 * dim :]], axis=0)

    def scores(d, state):
        top, total, delta = state
        contract = (((1,), (1,)), ((), ()))
        s = lax.dot_general(kv_ref[d, :, :dim], q, contract, preferred_element_type=jnp.float32)
        dp = lax.dot_general(kv_ref[d, :, dim:], g, contract, preferred_element_type=jnp.float32)
        k_pos = (my - d) * rows + lax.broadcasted_iota(jnp.int32, (rows, wide), 0)
        s = jnp.where((k_pos >= lo) & (k_pos <= pos), s, masked_value)
        new = jnp.maximum(top, jnp.max(s, axis=0, keepdims=True) * exp2_scale)
        p = jnp.exp2(s * exp2_scale - new)
        factor = jnp.exp2(top - new)
        s_ref[d] = p
        dp_ref[d] = dp
        top_ref[d] = new
        return (
            new,
            total * factor + jnp.sum(p, axis=0, keepdims=True),
            delta * factor + jnp.sum(p * dp, axis=0, keepdims=True),
        )

    zero = jnp.zeros((1, wide), jnp.float32)
    state = scores(0, (zero + masked_value, zero, zero))

    @pl.when(row >= 1)
    def _():
        arrived(8)

    to_second(start)
    along_first(start)

    def even_step(j, state):
        @pl.when(j != 4)
        def _():
            arrived(2 * j)

        to_partner(j, start)
        return scores(2 * j, state)

    even_end = jnp.minimum(order, 5) + 1
    state = lax.fori_loop(1, jnp.minimum(even_end, 3), even_step, state)

    @pl.when((row >= 2) & relays)
    def _():
        arrived(extra)

    along_second(start)
    state = lax.fori_loop(3, even_end, even_step, state)
    last = (core == 1) & (order >= 6)

    @pl.when(last)
    def _():
        arrived(12)
        slot_copy(12, 11, partner_send.at[6], place(row, chip, 0)).start()

    def odd_step(j, state):
        arrived(2 * j + 1)
        return scores(2 * j + 1, state)

    top, total, delta = lax.fori_loop(0, jnp.minimum(order + core, 6), odd_step, state)
    inverse = 1.0 / total
    delta = delta * inverse
    dq_ref[...] = jnp.zeros_like(dq_ref)

    def gradients(d):
        p = s_ref[d] * (jnp.exp2(top_ref[d] - top) * inverse)
        ds = (p * (dp_ref[d] - delta)).astype(jnp.bfloat16)
        dv = jnp.dot(p.astype(jnp.bfloat16), g, preferred_element_type=jnp.float32)
        dk = jnp.dot(ds, q, preferred_element_type=jnp.float32) * score_scale
        dq_ref[...] += lax.dot_general(
            kv_ref[d, :, :dim], ds, (((0,), (0,)), ((), ())), preferred_element_type=jnp.float32
        )
        return dk, dv

    def odd_copy(j):
        return remote(
            odd_ref.at[j],
            pair_ref.at[j],
            odd_send.at[j],
            pair_recv.at[j],
            place(row, chip, 1 - core),
        )

    def dispatch(k, act):
        @pl.when((k >= 1) & (k <= chip))
        def _():
            act(
                remote(
                    even_ref.at[k],
                    got_ref.at[k],
                    even_send.at[k],
                    got_recv.at[k],
                    place(row, chip - k, core),
                )
            )

        @pl.when((k > chip) & (k <= chip + 4) & (k != 4))
        def _():
            act(
                remote(
                    even_ref.at[k],
                    got_ref.at[4 + chip],
                    even_send.at[k],
                    got_recv.at[4 + chip],
                    place(row, chip - k + 4, core),
                )
            )

        @pl.when(k > chip + 4)
        def _():
            act(
                remote(
                    even_ref.at[k],
                    got_ref.at[8 + chip],
                    even_send.at[k],
                    got_recv.at[8 + chip],
                    place(row, chip - k + 8, core),
                )
            )

    def third(i, carry):
        j = jnp.minimum(order, 5) - i
        sends = (core == 1) | (j < order)
        gets = (core == 0) | (j < order)

        @pl.when(sends)
        def _():
            dk, dv = gradients(2 * j + 1)
            odd_ref[j, :, :dim] = dk.astype(jnp.bfloat16)
            odd_ref[j, :, dim:] = dv.astype(jnp.bfloat16)
            odd_copy(j).start()

        @pl.when(gets & (j + core <= 5))
        def _():
            dk, dv = gradients(2 * (j + core))
            odd_copy(j).wait_recv()
            even_ref[j + core, :, :dim] = (
                dk + pair_ref[j, :, :dim].astype(jnp.float32)
            ).astype(jnp.bfloat16)
            even_ref[j + core, :, dim:] = (
                dv + pair_ref[j, :, dim:].astype(jnp.float32)
            ).astype(jnp.bfloat16)
            dispatch(j + core, start)

        @pl.when(gets & (j + core == 6))
        def _():
            odd_copy(j).wait_recv()
            even_ref[6] = pair_ref[j]
            dispatch(6, start)

        return carry

    lax.fori_loop(0, jnp.minimum(even_end, 3), third, 0)

    acc = sum_ref

    def add(index):
        got(index)
        acc[...] += got_ref[index].astype(jnp.float32)

    def row_copy(index):
        return remote(
            row_ref.at[index],
            got_ref.at[10 + index],
            row_send.at[index],
            got_recv.at[10 + index],
            place(row - 1, chip, core),
        )

    @pl.when((row >= 2) & relays)
    def _():
        acc[...] = jnp.zeros((rows, 2 * dim), jnp.float32)
        for other in range(2):
            @pl.when(chip - 3 + core >= other)
            def _(other=other):
                add(8 + other)

        row_ref[1] = acc[...].astype(jnp.bfloat16)
        row_copy(1).start()

    lax.fori_loop(3, even_end, third, 0)

    @pl.when(core == 1)
    def _():
        dk, dv = gradients(0)
        even_ref[0, :, :dim] = dk.astype(jnp.bfloat16)
        even_ref[0, :, dim:] = dv.astype(jnp.bfloat16)

    dq = jnp.transpose(dq_ref[...] * score_scale)
    for part in range(2):
        dq_out_ref[:, :, part * dim : (part + 1) * dim] = (
            dq[part * rows : (part + 1) * rows].reshape(heads, chunk, dim).astype(jnp.bfloat16)
        )
    swap_start(2, dq_out_ref, dq_back_ref)

    @pl.when(row >= 1)
    def _():
        acc[...] = even_ref[4].astype(jnp.float32)
        for other in range(4):
            @pl.when((chip != other) & (chip + 1 + core >= other))
            def _(other=other):
                add(4 + other)

        @pl.when(has_next & relays)
        def _():
            add(11)

        row_ref[0] = acc[...].astype(jnp.bfloat16)
        row_copy(0).start()

    acc[...] = even_ref[0].astype(jnp.float32)
    for k in range(1, 4):
        @pl.when(chip + k <= 3)
        def _(k=k):
            add(k)

    @pl.when(has_next)
    def _():
        add(10)

    dkv_out_ref[...] = acc[...].reshape(heads, chunk, 2 * dim).astype(jnp.bfloat16)
    swap_start(3, dkv_out_ref, dkv_back_ref)

    to_next(sent)
    along_own(sent)
    to_second(sent)
    along_first(sent)
    along_second(sent)

    def sent_pair(j, carry):
        to_partner(j, sent)
        return carry

    lax.fori_loop(0, even_end, sent_pair, 0)

    @pl.when(last)
    def _():
        slot_copy(12, 11, partner_send.at[6], place(row, chip, 0)).wait_send()

    def sent_gradients(j, carry):
        @pl.when((core == 1) | (j < order))
        def _():
            odd_copy(j).wait_send()

        @pl.when((core == 0) | (j < order))
        def _():
            dispatch(j + core, sent)

        return carry

    lax.fori_loop(0, even_end, sent_gradients, 0)

    @pl.when((row >= 2) & relays)
    def _():
        row_copy(1).wait_send()

    @pl.when(row >= 1)
    def _():
        row_copy(0).wait_send()

    swap_sent(0, kv_out_ref, kv_in_ref)
    swap_sent(1, qg_out_ref, qg_in_ref)
    swap_sent(2, dq_out_ref, dq_back_ref)
    swap_sent(3, dkv_out_ref, dkv_back_ref)
    swap_arrived(2, dq_out_ref, dq_back_ref)
    swap_arrived(3, dkv_out_ref, dkv_back_ref)


def body(queries, keys, values, output_gradient, doc_lengths):
    chunk, kv_heads, dim = keys.shape
    group = queries.shape[1] // kv_heads
    rows = chunk * lax.axis_size("head")
    by_head = lambda parts: jnp.transpose(
        jnp.concatenate([part.reshape(chunk, kv_heads, -1) for part in parts], axis=2), (1, 0, 2)
    )
    kv = by_head([keys, values])
    qg = by_head([queries, output_gradient])
    reach = (WINDOW - 1) // rows + 2
    wide = group * rows
    vmem = pl.BlockSpec(memory_space=pltpu.VMEM)
    block = (rows, 2 * dim)
    swapped = (kv_heads, chunk, 2 * dim)
    low = jnp.bfloat16
    dma = pltpu.SemaphoreType.DMA
    dq, dkv = pl.pallas_call(
        attention_kernel,
        out_shape=(
            jax.ShapeDtypeStruct(swapped, low),
            jax.ShapeDtypeStruct(swapped, low),
        ),
        in_specs=[pl.BlockSpec(memory_space=pltpu.SMEM), vmem, vmem],
        out_specs=(vmem, vmem),
        scratch_shapes=[
            pltpu.VMEM(swapped, low),
            pltpu.VMEM((kv_heads, chunk, 4 * dim), low),
            pltpu.VMEM(swapped, low),
            pltpu.VMEM(swapped, low),
            pltpu.VMEM((14,) + block, low),
            pltpu.VMEM((reach, rows, wide), jnp.float32),
            pltpu.VMEM((reach, rows, wide), jnp.float32),
            pltpu.VMEM((reach, 1, wide), jnp.float32),
            pltpu.VMEM(block, jnp.float32),
            pltpu.VMEM((dim, wide), jnp.float32),
            pltpu.VMEM((6,) + block, low),
            pltpu.VMEM((7,) + block, low),
            pltpu.VMEM((6,) + block, low),
            pltpu.VMEM((12,) + block, low),
            pltpu.VMEM((2,) + block, low),
            dma((7,)),
            dma((2,)),
            dma((10,)),
            dma((14,)),
            dma((6,)),
            dma((7,)),
            dma((6,)),
            dma((2,)),
            dma((12,)),
            dma((4 * kv_heads,)),
            dma((4 * kv_heads,)),
        ],
        compiler_params=pltpu.CompilerParams(
            vmem_limit_bytes=60 * 2**20, collective_id=0, has_side_effects=True
        ),
        name="attention_backward",
    )(doc_lengths, kv, qg)
    by_token = lambda part: jnp.transpose(part, (1, 0, 2))
    return (
        by_token(dq).reshape(queries.shape),
        by_token(dkv[:, :, :dim]),
        by_token(dkv[:, :, dim:]),
    )


def solution(mesh):
    spec = P(("seq", "head"), None, None)
    return jax.shard_map(
        body,
        mesh=mesh,
        in_specs=(spec, spec, spec, spec, P()),
        out_specs=(spec, spec, spec),
        check_vma=False,
    )
```

```python
import math

import jax
import jax.numpy as jnp
from jax import lax
from jax.experimental import pallas as pl
from jax.experimental.pallas import tpu as pltpu
from jax.sharding import PartitionSpec as P

WINDOW = 4096

score_scale = 144.0 ** (-0.5)
exp2_scale = score_scale * math.log2(math.e)
masked_value = -1e30


def attention_kernel(
    lengths_ref, k_out_ref, v_out_ref, qg_out_ref, dq_back_ref, dkv_back_ref,
    k_in_ref, v_in_ref, qg_in_ref, dq_out_ref, dkv_out_ref, kv_ref, s_ref, dp_ref, top_ref, sum_ref, dq_ref, odd_ref, even_ref, pair_ref, got_ref, row_ref,
    partner_send, across_send, chip_send, slot_recv, odd_send, even_send, pair_recv, row_send, got_recv,
    swap_send, swap_recv,
):
    heads, chunk, dim = k_out_ref.shape
    rows = heads * chunk
    reach, _, wide = s_ref.shape
    my = lax.axis_index("seq")
    my_head = lax.axis_index("head")
    grid_rows = lax.axis_size("seq") // 8
    row = my // 8
    chip = my // 2 - row * 4
    core = my - (my // 2) * 2
    order = my // 2

    def place(r, x, c):
        return (r * 8 + x * 2 + c, my_head)

    def remote(source, target, send, recv, device):
        return pltpu.make_async_remote_copy(
            src_ref=source,
            dst_ref=target,
            send_sem=send,
            recv_sem=recv,
            device_id=device,
            device_id_type=pl.DeviceIdType.MESH,
        )

    def slot_copy(half, source, target, sends, index, device):
        return remote(
            kv_ref.at[half, source],
            kv_ref.at[half, target],
            sends.at[2 * index + half],
            slot_recv.at[2 * target + half],
            device,
        )

    def arrived(half, slot):
        slot_copy(half, slot, slot, chip_send, 0, place(row, chip, core)).wait_recv()

    def got(index):
        remote(
            got_ref.at[index],
            got_ref.at[index],
            row_send.at[0],
            got_recv.at[index],
            place(row, chip, core),
        ).wait_recv()

    extra = 13
    has_next = row < grid_rows - 1
    relays = chip >= 3 - core

    def to_next(half, act):
        @pl.when(has_next)
        def _():
            act(slot_copy(half, 0, 8, across_send, 0, place(row + 1, chip, core)))

    def to_second(half, act):
        @pl.when((row >= 1) & has_next & relays)
        def _():
            act(slot_copy(half, 8, extra, across_send, 1, place(row + 1, chip, core)))

    def along_own(half, act):
        for other in range(4):
            @pl.when(chip < other)
            def _(other=other):
                target = 2 * (other - chip)
                act(slot_copy(half, 0, target, chip_send, other, place(row, other, core)))

    def along_first(half, act):
        for other in range(4):
            @pl.when((row >= 1) & (chip != other) & (chip + 1 + core >= other))
            def _(other=other):
                target = 8 + 2 * (other - chip)
                act(slot_copy(half, 8, target, chip_send, 4 + other, place(row, other, core)))

    def along_second(half, act):
        for other in range(2):
            @pl.when((row >= 2) & (chip - 3 + core >= other))
            def _(other=other):
                target = 16 + 2 * (other - chip)
                act(
                    slot_copy(half, extra, target, chip_send, 8 + other, place(row, other, core))
                )

    def to_partner(half, j, act):
        @pl.when(core == 0)
        def _():
            act(slot_copy(half, 2 * j, 2 * j + 1, partner_send, j, place(row, chip, 1)))

        @pl.when((core == 1) & (j >= 1))
        def _():
            act(slot_copy(half, 2 * j, 2 * j - 1, partner_send, j, place(row, chip, 0)))

    def start(copy):
        copy.start()

    def sent(copy):
        copy.wait_send()

    def swap(n, source, target, peer):
        return remote(
            source.at[peer],
            target.at[my_head],
            swap_send.at[n * heads + peer],
            swap_recv.at[n * heads + my_head],
            (my, peer),
        )

    def swap_start(n, source, target):
        def one(step, carry):
            swap(n, source, target, (my_head + step) % heads).start()
            return carry

        lax.fori_loop(1, heads, one, 0)
        target[my_head] = source[my_head]

    def swap_arrived(n, source, target):
        def one(step, carry):
            peer = (my_head + step) % heads
            remote(
                source.at[peer],
                target.at[peer],
                swap_send.at[n * heads + peer],
                swap_recv.at[n * heads + peer],
                (my, peer),
            ).wait_recv()
            return carry

        lax.fori_loop(1, heads, one, 0)

    def swap_sent(n, source, target):
        def one(step, carry):
            swap(n, source, target, (my_head + step) % heads).wait_send()
            return carry

        lax.fori_loop(1, heads, one, 0)

    barrier = pltpu.get_barrier_semaphore()

    def greet(device):
        pl.semaphore_signal(
            barrier, inc=1, device_id=device, device_id_type=pl.DeviceIdType.MESH
        )

    for step in range(1, 4):
        greet(place(row, (chip + step) % 4, core))
    greet(place(row, chip, 1 - core))

    greet(place((row + 1) % grid_rows, chip, core))
    greet(place((row + grid_rows - 1) % grid_rows, chip, core))

    def greet_head(step, carry):
        greet((my, (my_head + step) % heads))
        return carry

    lax.fori_loop(1, heads, greet_head, 0)
    pl.semaphore_wait(barrier, 5 + heads)
    swap_start(0, k_out_ref, k_in_ref)
    swap_sent(0, k_out_ref, k_in_ref)
    swap_start(4, v_out_ref, v_in_ref)

    def begin(half, n, source, target):
        swap_arrived(n, source, target)
        kv_ref[half, 0] = target[...].astype(jnp.float32).reshape(rows, dim).astype(jnp.bfloat16)
        to_next(half, start)
        along_own(half, start)
        to_partner(half, 0, start)

    begin(0, 0, k_out_ref, k_in_ref)
    begin(1, 4, v_out_ref, v_in_ref)
    swap_start(1, qg_out_ref, qg_in_ref)
    for half in range(2):
        @pl.when(row >= 1)
        def _(half=half):
            arrived(half, 8)

        to_second(half, start)
        along_first(half, start)

    pos = my * rows + lax.broadcasted_iota(jnp.int32, (1, rows), 1)
    end = lengths_ref[0]
    lo = jnp.zeros((1, rows), jnp.int32)
    for document in range(1, lengths_ref.shape[0]):
        lo = jnp.where(pos >= end, end, lo)
        end = end + lengths_ref[document]
    lo = jnp.maximum(lo, pos - (WINDOW - 1))
    pos = jnp.concatenate([pos] * (wide // rows), axis=1)
    lo = jnp.concatenate([lo] * (wide // rows), axis=1)
    swap_arrived(1, qg_out_ref, qg_in_ref)
    qg = qg_in_ref[...].astype(jnp.float32).reshape(rows, 4 * dim).astype(jnp.bfloat16)
    q = jnp.concatenate([qg[:, :dim], qg[:, dim : 2 * dim]], axis=0)
    g = jnp.concatenate([qg[:, 2 * dim : 3 * dim], qg[:, 3 * dim :]], axis=0)

    def scores(d, state):
        top, total, delta = state
        contract = (((1,), (1,)), ((), ()))
        s = lax.dot_general(kv_ref[0, d], q, contract, preferred_element_type=jnp.float32)
        dp = lax.dot_general(kv_ref[1, d], g, contract, preferred_element_type=jnp.float32)
        k_pos = (my - d) * rows + lax.broadcasted_iota(jnp.int32, (rows, wide), 0)
        s = jnp.where((k_pos >= lo) & (k_pos <= pos), s, masked_value)
        new = jnp.maximum(top, jnp.max(s, axis=0, keepdims=True) * exp2_scale)
        p = jnp.exp2(s * exp2_scale - new)
        factor = jnp.exp2(top - new)
        s_ref[d] = p
        dp_ref[d] = dp
        top_ref[d] = new
        return (
            new,
            total * factor + jnp.sum(p, axis=0, keepdims=True),
            delta * factor + jnp.sum(p * dp, axis=0, keepdims=True),
        )

    zero = jnp.zeros((1, wide), jnp.float32)
    state = scores(0, (zero + masked_value, zero, zero))

    def even_step(j, state):
        for half in range(2):
            @pl.when(j != 4)
            def _(half=half):
                arrived(half, 2 * j)

            to_partner(half, j, start)

        return scores(2 * j, state)

    even_end = jnp.minimum(order, 5) + 1
    state = lax.fori_loop(1, jnp.minimum(even_end, 3), even_step, state)

    for half in range(2):
        @pl.when((row >= 2) & relays)
        def _(half=half):
            arrived(half, extra)

        along_second(half, start)

    state = lax.fori_loop(3, even_end, even_step, state)
    last = (core == 1) & (order >= 6)

    @pl.when(last)
    def _():
        for half in range(2):
            arrived(half, 12)
            slot_copy(half, 12, 11, partner_send, 6, place(row, chip, 0)).start()

    def odd_step(j, state):
        arrived(0, 2 * j + 1)
        arrived(1, 2 * j + 1)
        return scores(2 * j + 1, state)

    top, total, delta = lax.fori_loop(0, jnp.minimum(order + core, 6), odd_step, state)
    inverse = 1.0 / total
    delta = delta * inverse
    dq_ref[...] = jnp.zeros_like(dq_ref)

    def gradients(d):
        p = s_ref[d] * (jnp.exp2(top_ref[d] - top) * inverse)
        ds = (p * (dp_ref[d] - delta)).astype(jnp.bfloat16)
        dv = jnp.dot(p.astype(jnp.bfloat16), g, preferred_element_type=jnp.float32)
        dk = jnp.dot(ds, q, preferred_element_type=jnp.float32) * score_scale
        dq_ref[...] += lax.dot_general(
            kv_ref[0, d], ds, (((0,), (0,)), ((), ())), preferred_element_type=jnp.float32
        )
        return dk, dv

    def odd_copy(j):
        return remote(
            odd_ref.at[j],
            pair_ref.at[j],
            odd_send.at[j],
            pair_recv.at[j],
            place(row, chip, 1 - core),
        )

    def dispatch(k, act):
        @pl.when((k >= 1) & (k <= chip))
        def _():
            act(
                remote(
                    even_ref.at[k],
                    got_ref.at[k],
                    even_send.at[k],
                    got_recv.at[k],
                    place(row, chip - k, core),
                )
            )

        @pl.when((k > chip) & (k <= chip + 4) & (k != 4))
        def _():
            act(
                remote(
                    even_ref.at[k],
                    got_ref.at[4 + chip],
                    even_send.at[k],
                    got_recv.at[4 + chip],
                    place(row, chip - k + 4, core),
                )
            )

        @pl.when(k > chip + 4)
        def _():
            act(
                remote(
                    even_ref.at[k],
                    got_ref.at[8 + chip],
                    even_send.at[k],
                    got_recv.at[8 + chip],
                    place(row, chip - k + 8, core),
                )
            )

    def third(i, carry):
        j = jnp.minimum(order, 5) - i
        sends = (core == 1) | (j < order)
        gets = (core == 0) | (j < order)

        @pl.when(sends)
        def _():
            dk, dv = gradients(2 * j + 1)
            odd_ref[j, :, :dim] = dk.astype(jnp.bfloat16)
            odd_ref[j, :, dim:] = dv.astype(jnp.bfloat16)
            odd_copy(j).start()

        @pl.when(gets & (j + core <= 5))
        def _():
            dk, dv = gradients(2 * (j + core))
            odd_copy(j).wait_recv()
            even_ref[j + core, :, :dim] = (
                dk + pair_ref[j, :, :dim].astype(jnp.float32)
            ).astype(jnp.bfloat16)
            even_ref[j + core, :, dim:] = (
                dv + pair_ref[j, :, dim:].astype(jnp.float32)
            ).astype(jnp.bfloat16)
            dispatch(j + core, start)

        @pl.when(gets & (j + core == 6))
        def _():
            odd_copy(j).wait_recv()
            even_ref[6] = pair_ref[j]
            dispatch(6, start)

        return carry

    lax.fori_loop(0, jnp.minimum(even_end, 3), third, 0)

    acc = sum_ref

    def add(index):
        got(index)
        acc[...] += got_ref[index].astype(jnp.float32)

    def row_copy(index):
        return remote(
            row_ref.at[index],
            got_ref.at[10 + index],
            row_send.at[index],
            got_recv.at[10 + index],
            place(row - 1, chip, core),
        )

    @pl.when((row >= 2) & relays)
    def _():
        acc[...] = jnp.zeros((rows, 2 * dim), jnp.float32)
        for other in range(2):
            @pl.when(chip - 3 + core >= other)
            def _(other=other):
                add(8 + other)

        row_ref[1] = acc[...].astype(jnp.bfloat16)
        row_copy(1).start()

    lax.fori_loop(3, even_end, third, 0)

    @pl.when(core == 1)
    def _():
        dk, dv = gradients(0)
        even_ref[0, :, :dim] = dk.astype(jnp.bfloat16)
        even_ref[0, :, dim:] = dv.astype(jnp.bfloat16)

    dq = jnp.transpose(dq_ref[...] * score_scale)
    for part in range(2):
        dq_out_ref[:, :, part * dim : (part + 1) * dim] = (
            dq[part * rows : (part + 1) * rows].reshape(heads, chunk, dim).astype(jnp.bfloat16)
        )
    swap_start(2, dq_out_ref, dq_back_ref)

    @pl.when(row >= 1)
    def _():
        acc[...] = even_ref[4].astype(jnp.float32)
        for other in range(4):
            @pl.when((chip != other) & (chip + 1 + core >= other))
            def _(other=other):
                add(4 + other)

        @pl.when(has_next & relays)
        def _():
            add(11)

        row_ref[0] = acc[...].astype(jnp.bfloat16)
        row_copy(0).start()

    acc[...] = even_ref[0].astype(jnp.float32)
    for k in range(1, 4):
        @pl.when(chip + k <= 3)
        def _(k=k):
            add(k)

    @pl.when(has_next)
    def _():
        add(10)

    dkv_out_ref[...] = acc[...].reshape(heads, chunk, 2 * dim).astype(jnp.bfloat16)
    swap_start(3, dkv_out_ref, dkv_back_ref)

    for half in range(2):
        to_next(half, sent)
        along_own(half, sent)
        to_second(half, sent)
        along_first(half, sent)
        along_second(half, sent)

    def sent_pair(j, carry):
        to_partner(0, j, sent)
        to_partner(1, j, sent)
        return carry

    lax.fori_loop(0, even_end, sent_pair, 0)

    @pl.when(last)
    def _():
        for half in range(2):
            slot_copy(half, 12, 11, partner_send, 6, place(row, chip, 0)).wait_send()

    def sent_gradients(j, carry):
        @pl.when((core == 1) | (j < order))
        def _():
            odd_copy(j).wait_send()

        @pl.when((core == 0) | (j < order))
        def _():
            dispatch(j + core, sent)

        return carry

    lax.fori_loop(0, even_end, sent_gradients, 0)

    @pl.when((row >= 2) & relays)
    def _():
        row_copy(1).wait_send()

    @pl.when(row >= 1)
    def _():
        row_copy(0).wait_send()

    swap_sent(4, v_out_ref, v_in_ref)
    swap_sent(1, qg_out_ref, qg_in_ref)
    swap_sent(2, dq_out_ref, dq_back_ref)
    swap_sent(3, dkv_out_ref, dkv_back_ref)
    swap_arrived(2, dq_out_ref, dq_back_ref)
    swap_arrived(3, dkv_out_ref, dkv_back_ref)


def body(queries, keys, values, output_gradient, doc_lengths):
    chunk, kv_heads, dim = keys.shape
    group = queries.shape[1] // kv_heads
    rows = chunk * lax.axis_size("head")
    by_head = lambda parts: jnp.transpose(
        jnp.concatenate([part.reshape(chunk, kv_heads, -1) for part in parts], axis=2), (1, 0, 2)
    )
    k = by_head([keys])
    v = by_head([values])
    qg = by_head([queries, output_gradient])
    reach = (WINDOW - 1) // rows + 2
    wide = group * rows
    vmem = pl.BlockSpec(memory_space=pltpu.VMEM)
    block = (rows, 2 * dim)
    swapped = (kv_heads, chunk, 2 * dim)
    low = jnp.bfloat16
    dma = pltpu.SemaphoreType.DMA
    dq, dkv = pl.pallas_call(
        attention_kernel,
        out_shape=(
            jax.ShapeDtypeStruct(swapped, low),
            jax.ShapeDtypeStruct(swapped, low),
        ),
        in_specs=[pl.BlockSpec(memory_space=pltpu.SMEM), vmem, vmem, vmem],
        out_specs=(vmem, vmem),
        scratch_shapes=[
            pltpu.VMEM((kv_heads, chunk, dim), low),
            pltpu.VMEM((kv_heads, chunk, dim), low),
            pltpu.VMEM((kv_heads, chunk, 4 * dim), low),
            pltpu.VMEM(swapped, low),
            pltpu.VMEM(swapped, low),
            pltpu.VMEM((2, 14, rows, dim), low),
            pltpu.VMEM((reach, rows, wide), jnp.float32),
            pltpu.VMEM((reach, rows, wide), jnp.float32),
            pltpu.VMEM((reach, 1, wide), jnp.float32),
            pltpu.VMEM(block, jnp.float32),
            pltpu.VMEM((dim, wide), jnp.float32),
            pltpu.VMEM((6,) + block, low),
            pltpu.VMEM((7,) + block, low),
            pltpu.VMEM((6,) + block, low),
            pltpu.VMEM((12,) + block, low),
            pltpu.VMEM((2,) + block, low),
            dma((14,)),
            dma((4,)),
            dma((20,)),
            dma((28,)),
            dma((6,)),
            dma((7,)),
            dma((6,)),
            dma((2,)),
            dma((12,)),
            dma((5 * kv_heads,)),
            dma((5 * kv_heads,)),
        ],
        compiler_params=pltpu.CompilerParams(
            vmem_limit_bytes=60 * 2**20, collective_id=0, has_side_effects=True
        ),
        name="attention_backward",
    )(doc_lengths, k, v, qg)
    by_token = lambda part: jnp.transpose(part, (1, 0, 2))
    return (
        by_token(dq).reshape(queries.shape),
        by_token(dkv[:, :, :dim]),
        by_token(dkv[:, :, dim:]),
    )


def solution(mesh):
    spec = P(("seq", "head"), None, None)
    return jax.shard_map(
        body,
        mesh=mesh,
        in_specs=(spec, spec, spec, spec, P()),
        out_specs=(spec, spec, spec),
        check_vma=False,
    )
```
